32 devices in a mesh: chan: 16 (over z, y, core), band: 2 (over x).
Axes of the slice: x: 2, y: 2, z: 4, core: 2. Of those that a mesh axis runs over, the one named last changes fastest.
Arguments:
- strain: bfloat16 [4096, 4, 4096], P('chan', None, 'band'), may hold values from -6 to 6
- band_start: int32 [2], replicated, may hold values from 4 to 818
Outputs:
- coherency: bfloat16 [2, 2, 4096, 4096], P('band', None, 'chan')
The draws below stay inside these ranges and needn't reach their ends.
All inputs are finite; a program needn't handle non-finite values.
Results may differ from the reference program's by a relative error of at most 0.0056.
Values may be sent and summed in bfloat16 or wider, within the bound.
A program may use at most 64 MiB of HBM per device.

```python
import math
import jax
import jax.numpy as jnp
from jax import lax

WINDOW_SAMPLES = 4096
K = 32
WINDOWS = 4
FIBRE_CHANNELS = 4096
BANDS = 2


def steps_of(own_key, extent, cuts, smallest, largest):
    level = 1.0
    for dim, shards_of in cuts:
        draws = jax.random.uniform(jax.random.fold_in(jax.random.fold_in(own_key, 6), dim), (shards_of,), jnp.float32, smallest / len(cuts), largest / len(cuts))
        level = level * jnp.repeat(jnp.exp(draws), extent[dim] // shards_of).reshape((-1,) + (1,) * (len(extent) - 1 - dim))
    return level


def centred(rng, dims, deviation, most, shards=(), kind=jnp.bfloat16):
    entries = deviation * jax.random.normal(rng, dims, jnp.float32)
    if shards:
        entries = entries * steps_of(rng, dims, shards, -0.22, 0.18)
    return jnp.clip(entries, -most, most).astype(kind)


def setup_inputs(seed: int = 0) -> dict:
    key_list = jax.random.split(jax.random.key(seed), 3)
    strain = centred(key_list[0], (FIBRE_CHANNELS, WINDOWS, WINDOW_SAMPLES), 1.0, 6.0, ((0, 16), (2, 2)))
    band_start = jax.random.randint(key_list[1], (BANDS,), 4, WINDOW_SAMPLES // 5).astype(jnp.int32)
    return dict(strain=strain, band_start=band_start)


def build_fourier_table(first_bin):
    positions = jnp.arange(WINDOW_SAMPLES, dtype=jnp.int32)
    freqs = first_bin + jnp.arange(K, dtype=jnp.int32)
    phase_angles = positions[:, None] * freqs[None, :] % WINDOW_SAMPLES
    angles = phase_angles.astype(jnp.float32) * (2.0 * math.pi / WINDOW_SAMPLES)
    taper = 0.5 - 0.5 * jnp.cos(positions.astype(jnp.float32) * (2.0 * math.pi / WINDOW_SAMPLES))
    cosine = taper[:, None] * jnp.cos(angles)
    sine = -taper[:, None] * jnp.sin(angles)
    return jnp.concatenate([cosine, sine], axis=1).astype(jnp.bfloat16)

def one_band(strain, first_bin):
    table = build_fourier_table(first_bin)
    flat = strain.reshape(FIBRE_CHANNELS * WINDOWS, WINDOW_SAMPLES)
    spectrum = jnp.dot(flat, table, preferred_element_type=jnp.float32)
    power = lax.optimization_barrier(jnp.mean(spectrum * spectrum, axis=1, keepdims=True))
    whitened = (spectrum * lax.rsqrt(power + 1e-06)).astype(jnp.bfloat16)
    panel = whitened.reshape(FIBRE_CHANNELS, WINDOWS, 2, K).transpose(0, 2, 1, 3).reshape(FIBRE_CHANNELS, 2 * WINDOWS * K)
    half_feat = WINDOWS * K
    rotated = jnp.concatenate([-panel[:, half_feat:], panel[:, :half_feat]], axis=1)
    scale = 1.0 / (2.0 * K)
    real_out = (jnp.dot(panel, panel.T, preferred_element_type=jnp.float32) * scale).astype(jnp.bfloat16)
    imag_out = (jnp.dot(panel, rotated.T, preferred_element_type=jnp.float32) * scale).astype(jnp.bfloat16)
    return jnp.stack([real_out, imag_out])

def reference(strain, band_start):
    return lax.map(lambda first_bin: one_band(strain, first_bin), band_start)
```

```python
import functools
import math

import jax
import jax.numpy as jnp
from jax import lax
from jax.experimental import pallas as pl
from jax.experimental.pallas import tpu as pltpu
from jax.sharding import PartitionSpec as P

WINDOW_SAMPLES = 4096
K = 32
CHUNKS = 4
MESH = pl.DeviceIdType.MESH


def cos_turns(m):
    half, quarter = WINDOW_SAMPLES // 2, WINDOW_SAMPLES // 4
    t = (jnp.abs(m - half) - quarter).astype(jnp.float32) * (math.pi / half)
    z = t * t
    p = jnp.float32(1.0 / math.factorial(13))
    for order in (11, 9, 7, 5, 3, 1):
        sign = 1.0 if order % 4 == 1 else -1.0
        p = p * z + jnp.float32(sign / math.factorial(order))
    return p * t


def gather_kernel(
    n, nb, start_ref, x_hbm, g_ref, pq_ref,
    xbuf, tab, spec, own, xs, xr,
    in_sem, xs_sem, xr_sem, up_sem, down_sem, y_sem, core_sem, recv_sem,
):
    chans, windows, samp = xbuf.shape
    width = 2 * K
    cc = chans // CHUNKS
    cores = 2 if n % 2 == 0 else 1
    chips = n // cores
    inner = 2 if chips % 2 == 0 else 1
    outer = chips // inner
    me = lax.axis_index("chan")
    band = lax.axis_index("band")
    core = lax.rem(me, cores)
    chip = lax.div(me, cores)
    y = lax.rem(chip, inner)
    z = lax.div(chip, inner)

    def index(zz, yy, kk):
        return (zz * inner + yy) * cores + kk

    def load(k):
        rows = pl.ds(k * cc, cc)
        return pltpu.make_async_copy(x_hbm.at[rows], xbuf.at[rows], in_sem.at[k])

    for k in range(CHUNKS):
        load(k).start()

    barrier = pltpu.get_barrier_semaphore()
    up, down = index(z + 1, y, core), index(z - 1, y, core)
    y_peer, core_peer = index(z, inner - 1 - y, core), index(z, y, cores - 1 - core)
    has_up, has_down = z < outer - 1, z > 0
    for g in range(nb - 1):
        pl.semaphore_signal(
            barrier, inc=1, device_id={"band": lax.rem(band + 1 + g, nb)}, device_id_type=MESH
        )

    @pl.when(has_up)
    def _():
        pl.semaphore_signal(barrier, inc=1, device_id={"chan": up}, device_id_type=MESH)

    @pl.when(has_down)
    def _():
        pl.semaphore_signal(barrier, inc=1, device_id={"chan": down}, device_id_type=MESH)

    if inner > 1:
        pl.semaphore_signal(barrier, inc=1, device_id={"chan": y_peer}, device_id_type=MESH)
    if cores > 1:
        pl.semaphore_signal(barrier, inc=1, device_id={"chan": core_peer}, device_id_type=MESH)

    lane = lax.broadcasted_iota(jnp.int32, (1, nb * width), 1)
    freq = lane % K
    for g in range(nb):
        freq = freq + jnp.where(lane // width == g, start_ref[lax.rem(band + 1 + g, nb)], 0)
    shift = jnp.where((lane // K) % 2 == 1, WINDOW_SAMPLES // 4, 0)
    rows_at_once = min(256, samp)

    def fill(r, carry):
        base = pl.multiple_of(r * rows_at_once, rows_at_once)
        pos = band * samp + base + lax.broadcasted_iota(jnp.int32, (rows_at_once, nb * width), 0)
        taper = 0.5 - 0.5 * cos_turns(pos)
        m = (pos * freq + shift) & (WINDOW_SAMPLES - 1)
        tab[pl.ds(base, rows_at_once), :] = (taper * cos_turns(m)).astype(jnp.bfloat16)
        return carry

    lax.fori_loop(0, samp // rows_at_once, fill, 0)

    def band_copy(g, k):
        return pltpu.make_async_remote_copy(
            src_ref=xs.at[g, pl.ds(k * cc, cc)],
            dst_ref=xr.at[g, pl.ds(k * cc, cc)],
            send_sem=xs_sem.at[g, k],
            recv_sem=xr_sem.at[g, k],
            device_id={"band": lax.rem(band + 1 + g, nb)},
            device_id_type=MESH,
        )

    def send(src, k, sem, target):
        slot = g_ref.at[src, pl.ds(k * cc, cc)]
        return pltpu.make_async_remote_copy(
            src_ref=slot, dst_ref=slot, send_sem=sem, recv_sem=recv_sem.at[src, k],
            device_id={"chan": target}, device_id_type=MESH,
        )

    def send_up(d, k):
        return send(index(z - d, y, core), k, up_sem.at[d, k], up)

    def send_down(d, k):
        return send(index(z + d, y, core), k, down_sem.at[d, k], down)

    def send_y(d, k):
        return send(index(z + d, y, core), k, y_sem.at[d + outer - 1, k], y_peer)

    def send_core(far, d, k):
        yy = inner - 1 - y if far else y
        return send(index(z + d, yy, core), k, core_sem.at[far, d + outer - 1, k], core_peer)

    def in_line(d):
        return jnp.logical_and(z + d >= 0, z + d < outer)

    def arrived(zz, yy, kk, k):
        src = index(zz, yy, kk)
        send(src, k, y_sem.at[0, 0], y_peer if inner > 1 else core_peer).wait_recv()

    for k in range(CHUNKS):
        load(k).wait()
        x = xbuf[pl.ds(k * cc, cc)].reshape(cc * windows, samp)
        sums = jnp.dot(x, tab[...], preferred_element_type=jnp.float32)
        tiles, _, lanes = spec.shape
        for t in range(tiles):
            spec[t] = sums[:, t * lanes : (t + 1) * lanes]
        per_tile = lanes // width
        for g in range(nb):
            t, at = g // per_tile, g % per_tile * width
            parts = [spec[t, pl.ds(w, cc, stride=windows), :] for w in range(windows)]
            packed = jnp.concatenate([p[:, at : at + width] for p in parts], axis=1)
            if g < nb - 1:
                xs[g, pl.ds(k * cc, cc), :] = packed
            else:
                own[pl.ds(k * cc, cc), :] = packed
        if k == 0:
            pl.semaphore_wait(
                barrier,
                nb - 1 + (inner - 1) + (cores - 1) + has_up.astype(jnp.int32) + has_down.astype(jnp.int32),
            )
        for g in range(nb - 1):
            band_copy(g, k).start()

    def own_chunk(k):
        rows = pl.ds(k * cc, cc)
        total = own[rows, :]
        for g in range(nb - 1):
            band_copy(g, k).wait_recv()
            total = total + xr[g, rows, :]
        white = []
        for w in range(windows):
            s = total[:, w * width : (w + 1) * width]
            power = jnp.sum(s * s, axis=1, keepdims=True) * (1.0 / width)
            white.append(s * lax.rsqrt(power + 1e-06))
        panel = jnp.concatenate(white, axis=1)
        g_ref[me, rows, :] = panel.astype(jnp.bfloat16)

        @pl.when(has_up)
        def _():
            send_up(0, k).start()

        @pl.when(has_down)
        def _():
            send_down(0, k).start()

        if inner > 1:
            send_y(0, k).start()
        if cores > 1:
            send_core(0, 0, k).start()
        feats = panel.shape[1]
        is_real = lax.broadcasted_iota(jnp.int32, panel.shape, 1) % width < K
        rotated = jnp.where(
            is_real, pltpu.roll(panel, feats - K, axis=1), -pltpu.roll(panel, K, axis=1)
        )
        pq_ref[0, rows, :] = panel.astype(jnp.bfloat16)
        pq_ref[1, rows, :] = rotated.astype(jnp.bfloat16)

    def line_chunk(d, k):
        @pl.when(in_line(d))
        def _():
            arrived(z + d, y, core, k)
            if d < 0:
                pl.when(has_up)(lambda: send_up(-d, k).start())
            else:
                pl.when(has_down)(lambda: send_down(d, k).start())
            if inner > 1:
                send_y(d, k).start()
            if cores > 1:
                send_core(0, d, k).start()

    def far_chunk(d, k):
        @pl.when(in_line(d))
        def _():
            arrived(z + d, inner - 1 - y, core, k)
            if cores > 1:
                send_core(1, d, k).start()

    events = []
    for k in range(CHUNKS):
        events.append((1.4 * k, 0, own_chunk, (k,)))
        for d in range(1, outer):
            for s in (-d, d):
                events.append((1.4 * k + 2.2 * d, 1, line_chunk, (s, k)))
        if inner > 1:
            for d in range(outer):
                for s in {-d, d}:
                    events.append((1.4 * k + 2.2 * d + 2.3, 2, far_chunk, (s, k)))
    for _, _, run, args in sorted(events, key=lambda e: (e[0], e[1], e[3])):
        run(*args)

    if cores > 1:
        for k in range(CHUNKS):
            for yy in range(inner):
                for zz in range(outer):
                    arrived(zz, yy, cores - 1 - core, k)

    for k in range(CHUNKS):
        for g in range(nb - 1):
            band_copy(g, k).wait_send()
        for d in range(outer):
            pl.when(jnp.logical_and(in_line(-d), has_up))(lambda: send_up(d, k).wait_send())
            pl.when(jnp.logical_and(in_line(d), has_down))(lambda: send_down(d, k).wait_send())
        for d in range(1 - outer, outer):
            @pl.when(in_line(d))
            def _():
                if inner > 1:
                    send_y(d, k).wait_send()
                if cores > 1:
                    for far in range(inner):
                        send_core(far, d, k).wait_send()


def gather_panels(n, nb, strain, band_start):
    chans, windows, samp = strain.shape
    width = 2 * K
    feats = windows * width
    outer = n
    for _ in range(2):
        outer = outer // 2 if outer % 2 == 0 else outer
    dma = pltpu.SemaphoreType.DMA
    return pl.pallas_call(
        functools.partial(gather_kernel, n, nb),
        out_shape=(
            jax.ShapeDtypeStruct((n, chans, feats), jnp.bfloat16),
            jax.ShapeDtypeStruct((2, chans, feats), jnp.bfloat16),
        ),
        in_specs=[
            pl.BlockSpec(memory_space=pltpu.SMEM),
            pl.BlockSpec(memory_space=pl.ANY),
        ],
        out_specs=(
            pl.BlockSpec(memory_space=pltpu.VMEM),
            pl.BlockSpec(memory_space=pltpu.VMEM),
        ),
        scratch_shapes=[
            pltpu.VMEM((chans, windows, samp), jnp.bfloat16),
            pltpu.VMEM((samp, nb * width), jnp.bfloat16),
            pltpu.VMEM((nb * width // 128, chans // CHUNKS * windows, 128), jnp.float32),
            pltpu.VMEM((chans, feats), jnp.float32),
            pltpu.VMEM((nb - 1, chans, feats), jnp.float32),
            pltpu.VMEM((nb - 1, chans, feats), jnp.float32),
            dma((CHUNKS,)),
            dma((nb - 1, CHUNKS)),
            dma((nb - 1, CHUNKS)),
            dma((outer, CHUNKS)),
            dma((outer, CHUNKS)),
            dma((2 * outer - 1, CHUNKS)),
            dma((2, 2 * outer - 1, CHUNKS)),
            dma((n, CHUNKS)),
        ],
        compiler_params=pltpu.CompilerParams(
            collective_id=0, has_side_effects=True, vmem_limit_bytes=48 << 20
        ),
    )(band_start, strain)


def gram_kernel(pq_ref, g_ref, o_ref):
    two, chans, feats = pq_ref.shape
    product = lax.dot_general(
        pq_ref[...].reshape(two * chans, feats),
        g_ref[...],
        (((1,), (1,)), ((), ())),
        preferred_element_type=jnp.float32,
    )
    o_ref[...] = (product * (1.0 / (2.0 * K))).astype(jnp.bfloat16).reshape(o_ref.shape)


def gram(pq, panels):
    two, chans, feats = pq.shape
    total = panels.shape[0]
    cols = min(512, total)
    return pl.pallas_call(
        gram_kernel,
        out_shape=jax.ShapeDtypeStruct((1, two, chans, total), jnp.bfloat16),
        grid=(total // cols,),
        in_specs=[
            pl.BlockSpec((two, chans, feats), lambda i: (0, 0, 0)),
            pl.BlockSpec((cols, feats), lambda i: (i, 0)),
        ],
        out_specs=pl.BlockSpec((1, two, chans, cols), lambda i: (0, 0, 0, i)),
    )(pq, panels)


def shards(n, nb, strain, band_start):
    panels, pq = gather_panels(n, nb, strain, band_start)
    return gram(pq, panels.reshape(-1, panels.shape[2]))


def solution(mesh):
    return jax.shard_map(
        functools.partial(shards, mesh.shape["chan"], mesh.shape["band"]),
        mesh=mesh,
        in_specs=(P("chan", None, "band"), P()),
        out_specs=P("band", None, "chan", None),
        check_vma=False,
    )
```

```python
import functools
import math

import jax
import jax.numpy as jnp
from jax import lax
from jax.experimental import pallas as pl
from jax.experimental.pallas import tpu as pltpu
from jax.sharding import PartitionSpec as P

WINDOW_SAMPLES = 4096
K = 32
CHUNKS = 4
PAIR = 2
MESH = pl.DeviceIdType.MESH


def cos_turns(m):
    half, quarter = WINDOW_SAMPLES // 2, WINDOW_SAMPLES // 4
    t = (jnp.abs(m - half) - quarter).astype(jnp.float32) * (math.pi / half)
    z = t * t
    p = jnp.float32(1.0 / math.factorial(13))
    for order in (11, 9, 7, 5, 3, 1):
        sign = 1.0 if order % 4 == 1 else -1.0
        p = p * z + jnp.float32(sign / math.factorial(order))
    return p * t


def gather_kernel(
    n, nb, start_ref, x_hbm, o_ref,
    xbuf, trig, bases, tab, spec, own, xs, xr, g_ref, pq_ref,
    in_sem, xs_sem, xr_sem, up_sem, down_sem, y_sem, core_sem, recv_sem,
):
    chans, windows, samp = xbuf.shape
    width = 2 * K
    cc = chans // CHUNKS
    cores = 2 if n % 2 == 0 else 1
    chips = n // cores
    inner = 2 if chips % 2 == 0 else 1
    outer = chips // inner
    me = lax.axis_index("chan")
    band = lax.axis_index("band")
    core = lax.rem(me, cores)
    chip = lax.div(me, cores)
    y = lax.rem(chip, inner)
    z = lax.div(chip, inner)

    def index(zz, yy, kk):
        return (zz * inner + yy) * cores + kk

    def load(k):
        rows = pl.ds(k * cc, cc)
        return pltpu.make_async_copy(x_hbm.at[rows], xbuf.at[rows], in_sem.at[k])

    for k in range(CHUNKS):
        load(k).start()

    barrier = pltpu.get_barrier_semaphore()
    up, down = index(z + 1, y, core), index(z - 1, y, core)
    y_peer, core_peer = index(z, inner - 1 - y, core), index(z, y, cores - 1 - core)
    has_up, has_down = z < outer - 1, z > 0
    for g in range(nb - 1):
        pl.semaphore_signal(
            barrier, inc=1, device_id={"band": lax.rem(band + 1 + g, nb)}, device_id_type=MESH
        )

    @pl.when(has_up)
    def _():
        pl.semaphore_signal(barrier, inc=1, device_id={"chan": up}, device_id_type=MESH)

    @pl.when(has_down)
    def _():
        pl.semaphore_signal(barrier, inc=1, device_id={"chan": down}, device_id_type=MESH)

    if inner > 1:
        pl.semaphore_signal(barrier, inc=1, device_id={"chan": y_peer}, device_id_type=MESH)
    if cores > 1:
        pl.semaphore_signal(barrier, inc=1, device_id={"chan": core_peer}, device_id_type=MESH)

    lane = lax.broadcasted_iota(jnp.int32, (1, nb * width), 1)
    freq = lane % K
    for g in range(nb):
        freq = freq + jnp.where(lane // width == g, start_ref[lax.rem(band + 1 + g, nb)], 0)
    shift = jnp.where((lane // K) % 2 == 1, WINDOW_SAMPLES // 4, 0)
    step = trig.shape[1]
    steps = samp // step
    offset = lax.broadcasted_iota(jnp.int32, (step, nb * width), 0)
    base = band * samp + step * lax.broadcasted_iota(jnp.int32, (steps, nb * width), 0)
    wrap, lag = WINDOW_SAMPLES - 1, 3 * (WINDOW_SAMPLES // 4)
    angle = offset * freq + shift
    trig[0] = cos_turns(angle & wrap)
    trig[1] = cos_turns((angle + lag) & wrap)
    trig[2] = 0.5 * cos_turns(offset & wrap)
    trig[3] = 0.5 * cos_turns((offset + lag) & wrap)
    angle = base * freq
    bases[0] = cos_turns(angle & wrap)
    bases[1] = cos_turns((angle + lag) & wrap)
    bases[2] = cos_turns(base & wrap)
    bases[3] = cos_turns((base + lag) & wrap)

    def fill(r, carry):
        turn = [bases[i, pl.ds(r, 1), :] for i in range(4)]
        taper = 0.5 - (trig[2] * turn[2] - trig[3] * turn[3])
        wave = trig[0] * turn[0] - trig[1] * turn[1]
        tab[pl.ds(pl.multiple_of(r * step, step), step), :] = (taper * wave).astype(jnp.bfloat16)
        return carry

    lax.fori_loop(0, steps, fill, 0, unroll=2)

    def band_copy(g, k):
        return pltpu.make_async_remote_copy(
            src_ref=xs.at[g, pl.ds(k * cc, cc)],
            dst_ref=xr.at[g, pl.ds(k * cc, cc)],
            send_sem=xs_sem.at[g, k],
            recv_sem=xr_sem.at[g, k],
            device_id={"band": lax.rem(band + 1 + g, nb)},
            device_id_type=MESH,
        )

    def send(src, k, sem, target):
        slot = g_ref.at[src, pl.ds(k * cc, cc)]
        return pltpu.make_async_remote_copy(
            src_ref=slot, dst_ref=slot, send_sem=sem, recv_sem=recv_sem.at[src, k],
            device_id={"chan": target}, device_id_type=MESH,
        )

    def send_up(d, k):
        return send(index(z - d, y, core), k, up_sem.at[d, k], up)

    def send_down(d, k):
        return send(index(z + d, y, core), k, down_sem.at[d, k], down)

    def send_y(d, k):
        return send(index(z + d, y, core), k, y_sem.at[d + outer - 1, k], y_peer)

    def send_core(far, d, k):
        yy = inner - 1 - y if far else y
        return send(index(z + d, yy, core), k, core_sem.at[far, d + outer - 1, k], core_peer)

    def in_line(d):
        return jnp.logical_and(z + d >= 0, z + d < outer)

    def arrived(zz, yy, kk, k):
        src = index(zz, yy, kk)
        send(src, k, y_sem.at[0, 0], y_peer if inner > 1 else core_peer).wait_recv()

    for k in range(CHUNKS):
        load(k).wait()
        x = xbuf[pl.ds(k * cc, cc)].reshape(cc * windows, samp)
        sums = jnp.dot(x, tab[...], preferred_element_type=jnp.float32)
        tiles, _, lanes = spec.shape
        for t in range(tiles):
            spec[t] = sums[:, t * lanes : (t + 1) * lanes]
        per_tile = lanes // width
        for g in range(nb):
            t, at = g // per_tile, g % per_tile * width
            parts = [spec[t, pl.ds(w, cc, stride=windows), :] for w in range(windows)]
            packed = jnp.concatenate([p[:, at : at + width] for p in parts], axis=1)
            if g < nb - 1:
                xs[g, pl.ds(k * cc, cc), :] = packed
            else:
                own[pl.ds(k * cc, cc), :] = packed
        if k == 0:
            pl.semaphore_wait(
                barrier,
                nb - 1 + (inner - 1) + (cores - 1) + has_up.astype(jnp.int32) + has_down.astype(jnp.int32),
            )
        for g in range(nb - 1):
            band_copy(g, k).start()

    def own_chunk(k):
        rows = pl.ds(k * cc, cc)
        total = own[rows, :]
        for g in range(nb - 1):
            band_copy(g, k).wait_recv()
            total = total + xr[g, rows, :]
        white = []
        for w in range(windows):
            s = total[:, w * width : (w + 1) * width]
            power = jnp.sum(s * s, axis=1, keepdims=True) * (1.0 / width)
            white.append(s * lax.rsqrt(power + 1e-06))
        panel = jnp.concatenate(white, axis=1)
        g_ref[me, rows, :] = panel.astype(jnp.bfloat16)

        @pl.when(has_up)
        def _():
            send_up(0, k).start()

        @pl.when(has_down)
        def _():
            send_down(0, k).start()

        if inner > 1:
            send_y(0, k).start()
        if cores > 1:
            send_core(0, 0, k).start()
        feats = panel.shape[1]
        is_real = lax.broadcasted_iota(jnp.int32, panel.shape, 1) % width < K
        rotated = jnp.where(
            is_real, pltpu.roll(panel, feats - K, axis=1), -pltpu.roll(panel, K, axis=1)
        )
        pq_ref[0, rows, :] = panel.astype(jnp.bfloat16)
        pq_ref[1, rows, :] = rotated.astype(jnp.bfloat16)

    def line_chunk(d, k):
        @pl.when(in_line(d))
        def _():
            arrived(z + d, y, core, k)
            if d < 0:
                pl.when(has_up)(lambda: send_up(-d, k).start())
            else:
                pl.when(has_down)(lambda: send_down(d, k).start())
            if inner > 1:
                send_y(d, k).start()
            if cores > 1:
                send_core(0, d, k).start()

    def far_chunk(d, k):
        @pl.when(in_line(d))
        def _():
            arrived(z + d, inner - 1 - y, core, k)
            if cores > 1:
                send_core(1, d, k).start()

    def gram(src, h):
        cols = PAIR * cc
        two, _, feats = pq_ref.shape
        product = lax.dot_general(
            pq_ref[...].reshape(two * chans, feats),
            g_ref[src, pl.ds(h * cols, cols), :],
            (((1,), (1,)), ((), ())),
            preferred_element_type=jnp.float32,
        )
        product = (product * (1.0 / width)).astype(jnp.bfloat16)
        at = pl.ds(pl.multiple_of(src * chans + h * cols, cols), cols)
        for i in range(two):
            o_ref[i, :, at] = product[i * chans : (i + 1) * chans]

    def near_gram(d, h):
        pl.when(in_line(d))(lambda: gram(index(z + d, y, core), h))

    def far_gram(d, h):
        pl.when(in_line(d))(lambda: gram(index(z + d, inner - 1 - y, core), h))

    def peer_gram(far, d, h):
        @pl.when(in_line(d))
        def _():
            yy = inner - 1 - y if far else y
            for k in range(PAIR * h, PAIR * h + PAIR):
                arrived(z + d, yy, cores - 1 - core, k)
            gram(index(z + d, yy, cores - 1 - core), h)

    hop, wire, gap, cost = 1.6, 0.7, 1.4, 0.3
    moves, jobs = [], []
    near, far = {}, {}
    for k in range(CHUNKS):
        for d in range(outer):
            near[d, k] = gap * k + (hop + wire) * d
    free = 0.0
    for d, k in sorted(near, key=lambda e: (near[e], e)):
        free = max(free, near[d, k]) + wire
        far[d, k] = free + hop
    for (d, k), t in near.items():
        if d == 0:
            moves.append((t, 0, own_chunk, (k,)))
        else:
            moves += [(t, 1, line_chunk, (s, k)) for s in (-d, d)]
    if inner > 1:
        for (d, k), t in far.items():
            moves += [(t, 2, far_chunk, (s, k)) for s in sorted({-d, d})]
    ready = near[0, CHUNKS - 1]
    for h in range(CHUNKS // PAIR):
        last = PAIR * h + PAIR - 1
        for d in range(outer):
            for s in sorted({-d, d}):
                jobs.append((max(ready, near[d, last]), 0, near_gram, (s, h)))
                if inner > 1:
                    jobs.append((max(ready, far[d, last]), 1, far_gram, (s, h)))
                if cores > 1:
                    for f, times in enumerate((near, far)[:inner]):
                        jobs.append((max(ready, times[d, last] + hop), 2, peer_gram, (f, s, h)))
    order = lambda e: (e[0], e[1], e[3])
    moves.sort(key=order)
    jobs.sort(key=order)
    now = 0.0
    for t, _, run, args in moves:
        while jobs and jobs[0][0] <= now and now + cost <= t:
            _, _, job, what = jobs.pop(0)
            job(*what)
            now += cost / 2
        run(*args)
        now = max(now, t)
    for _, _, job, what in jobs:
        job(*what)

    for k in range(CHUNKS):
        for g in range(nb - 1):
            band_copy(g, k).wait_send()
        for d in range(outer):
            pl.when(jnp.logical_and(in_line(-d), has_up))(lambda: send_up(d, k).wait_send())
            pl.when(jnp.logical_and(in_line(d), has_down))(lambda: send_down(d, k).wait_send())
        for d in range(1 - outer, outer):
            @pl.when(in_line(d))
            def _():
                if inner > 1:
                    send_y(d, k).wait_send()
                if cores > 1:
                    for far in range(inner):
                        send_core(far, d, k).wait_send()


def cross_spectra(n, nb, strain, band_start):
    chans, windows, samp = strain.shape
    width = 2 * K
    feats = windows * width
    outer = n
    for _ in range(2):
        outer = outer // 2 if outer % 2 == 0 else outer
    dma = pltpu.SemaphoreType.DMA
    return pl.pallas_call(
        functools.partial(gather_kernel, n, nb),
        out_shape=jax.ShapeDtypeStruct((2, chans, n * chans), jnp.bfloat16),
        in_specs=[
            pl.BlockSpec(memory_space=pltpu.SMEM),
            pl.BlockSpec(memory_space=pl.ANY),
        ],
        out_specs=pl.BlockSpec(memory_space=pltpu.VMEM),
        scratch_shapes=[
            pltpu.VMEM((chans, windows, samp), jnp.bfloat16),
            pltpu.VMEM((4, min(64, samp), nb * width), jnp.float32),
            pltpu.VMEM((4, samp // min(64, samp), nb * width), jnp.float32),
            pltpu.VMEM((samp, nb * width), jnp.bfloat16),
            pltpu.VMEM((nb * width // 128, chans // CHUNKS * windows, 128), jnp.float32),
            pltpu.VMEM((chans, feats), jnp.float32),
            pltpu.VMEM((nb - 1, chans, feats), jnp.float32),
            pltpu.VMEM((nb - 1, chans, feats), jnp.float32),
            pltpu.VMEM((n, chans, feats), jnp.bfloat16),
            pltpu.VMEM((2, chans, feats), jnp.bfloat16),
            dma((CHUNKS,)),
            dma((nb - 1, CHUNKS)),
            dma((nb - 1, CHUNKS)),
            dma((outer, CHUNKS)),
            dma((outer, CHUNKS)),
            dma((2 * outer - 1, CHUNKS)),
            dma((2, 2 * outer - 1, CHUNKS)),
            dma((n, CHUNKS)),
        ],
        compiler_params=pltpu.CompilerParams(
            collective_id=0, has_side_effects=True, vmem_limit_bytes=48 << 20
        ),
    )(band_start, strain)


def write_kernel(pieces, held, out, sem):
    two, chans, _ = held.shape
    rows = chans // pieces
    copies = []
    for i in range(two):
        for p in range(pieces):
            at = pl.ds(p * rows, rows)
            copies.append(pltpu.make_async_copy(held.at[i, at], out.at[0, i, at], sem.at[i, p]))
    for copy in copies:
        copy.start()
    for copy in copies:
        copy.wait()


def write_out(held):
    pieces = 8
    return pl.pallas_call(
        functools.partial(write_kernel, pieces),
        out_shape=jax.ShapeDtypeStruct((1,) + held.shape, held.dtype),
        in_specs=[pl.BlockSpec(memory_space=pl.ANY)],
        out_specs=pl.BlockSpec(memory_space=pl.ANY),
        scratch_shapes=[pltpu.SemaphoreType.DMA((held.shape[0], pieces))],
        compiler_params=pltpu.CompilerParams(vmem_limit_bytes=1 << 20),
    )(held)


def shards(n, nb, strain, band_start):
    return write_out(cross_spectra(n, nb, strain, band_start))


def solution(mesh):
    return jax.shard_map(
        functools.partial(shards, mesh.shape["chan"], mesh.shape["band"]),
        mesh=mesh,
        in_specs=(P("chan", None, "band"), P()),
        out_specs=P("band", None, "chan", None),
        check_vma=False,
    )
```

```python
import functools
import math

import jax
import jax.numpy as jnp
from jax import lax
from jax.experimental import pallas as pl
from jax.experimental.pallas import tpu as pltpu
from jax.sharding import PartitionSpec as P

WINDOW_SAMPLES = 4096
K = 32
EIGHTHS = (1, 1, 2, 2, 2)
CHUNKS = len(EIGHTHS)
GROUPS = ((0, 1, 2), (3, 4))
DETOUR = (2, 4)
MESH = pl.DeviceIdType.MESH


def cos_turns(m):
    half, quarter = WINDOW_SAMPLES // 2, WINDOW_SAMPLES // 4
    t = (jnp.abs(m - half) - quarter).astype(jnp.float32) * (math.pi / half)
    z = t * t
    p = jnp.float32(1.0 / math.factorial(13))
    for order in (11, 9, 7, 5, 3, 1):
        sign = 1.0 if order % 4 == 1 else -1.0
        p = p * z + jnp.float32(sign / math.factorial(order))
    return p * t


def gather_kernel(
    n, nb, start_hbm, x_hbm, o_ref,
    xbuf, trig, bases, tab, spec, own, xs, xr, g_ref, pq_ref,
    start_ref, start_sem, in_sem, xs_sem, xr_sem, up_sem, down_sem, y_sem, core_sem, detour_sem, recv_sem,
):
    chans, windows, samp = xbuf.shape
    width = 2 * K
    sizes = [chans * e // 8 for e in EIGHTHS]
    starts = [sum(sizes[:k]) for k in range(CHUNKS)]

    def rows_of(k):
        return pl.ds(starts[k], sizes[k])

    cores = 2 if n % 2 == 0 else 1
    chips = n // cores
    inner = 2 if chips % 2 == 0 else 1
    outer = chips // inner
    me = lax.axis_index("chan")
    band = lax.axis_index("band")
    core = lax.rem(me, cores)
    chip = lax.div(me, cores)
    y = lax.rem(chip, inner)
    z = lax.div(chip, inner)

    def index(zz, yy, kk):
        return (zz * inner + yy) * cores + kk

    detour = inner > 1 and outer % 2 == 0
    buddy = z + 1 - 2 * lax.rem(z, 2)

    def load(k):
        rows = rows_of(k)
        return pltpu.make_async_copy(x_hbm.at[rows], xbuf.at[rows], in_sem.at[k])

    for k in range(CHUNKS):
        load(k).start()
    first_bins = pltpu.make_async_copy(start_hbm, start_ref, start_sem)
    first_bins.start()

    barrier = pltpu.get_barrier_semaphore()
    up, down = index(z + 1, y, core), index(z - 1, y, core)
    y_peer, core_peer = index(z, inner - 1 - y, core), index(z, y, cores - 1 - core)
    has_up, has_down = z < outer - 1, z > 0
    for g in range(nb - 1):
        pl.semaphore_signal(
            barrier, inc=1, device_id={"band": lax.rem(band + 1 + g, nb)}, device_id_type=MESH
        )

    @pl.when(has_up)
    def _():
        pl.semaphore_signal(barrier, inc=1, device_id={"chan": up}, device_id_type=MESH)

    @pl.when(has_down)
    def _():
        pl.semaphore_signal(barrier, inc=1, device_id={"chan": down}, device_id_type=MESH)

    if inner > 1:
        pl.semaphore_signal(barrier, inc=1, device_id={"chan": y_peer}, device_id_type=MESH)
    if cores > 1:
        pl.semaphore_signal(barrier, inc=1, device_id={"chan": core_peer}, device_id_type=MESH)

    first_bins.wait()
    lane = lax.broadcasted_iota(jnp.int32, (1, nb * width), 1)
    freq = lane % K
    for g in range(nb):
        freq = freq + jnp.where(lane // width == g, start_ref[lax.rem(band + 1 + g, nb)], 0)
    shift = jnp.where((lane // K) % 2 == 1, WINDOW_SAMPLES // 4, 0)
    step = trig.shape[1]
    steps = samp // step
    offset = lax.broadcasted_iota(jnp.int32, (step, nb * width), 0)
    base = band * samp + step * lax.broadcasted_iota(jnp.int32, (steps, nb * width), 0)
    wrap, lag = WINDOW_SAMPLES - 1, 3 * (WINDOW_SAMPLES // 4)
    angle = offset * freq + shift
    trig[0] = cos_turns(angle & wrap)
    trig[1] = cos_turns((angle + lag) & wrap)
    trig[2] = 0.5 * cos_turns(offset & wrap)
    trig[3] = 0.5 * cos_turns((offset + lag) & wrap)
    angle = base * freq
    bases[0] = cos_turns(angle & wrap)
    bases[1] = cos_turns((angle + lag) & wrap)
    bases[2] = cos_turns(base & wrap)
    bases[3] = cos_turns((base + lag) & wrap)

    def fill(r, carry):
        turn = [bases[i, pl.ds(r, 1), :] for i in range(4)]
        taper = 0.5 - (trig[2] * turn[2] - trig[3] * turn[3])
        wave = trig[0] * turn[0] - trig[1] * turn[1]
        tab[pl.ds(pl.multiple_of(r * step, step), step), :] = (taper * wave).astype(jnp.bfloat16)
        return carry

    lax.fori_loop(0, steps, fill, 0, unroll=2)

    def band_copy(g, k):
        return pltpu.make_async_remote_copy(
            src_ref=xs.at[g, rows_of(k)],
            dst_ref=xr.at[g, rows_of(k)],
            send_sem=xs_sem.at[g, k],
            recv_sem=xr_sem.at[g, k],
            device_id={"band": lax.rem(band + 1 + g, nb)},
            device_id_type=MESH,
        )

    def send(src, k, sem, target):
        slot = g_ref.at[src, rows_of(k)]
        return pltpu.make_async_remote_copy(
            src_ref=slot, dst_ref=slot, send_sem=sem, recv_sem=recv_sem.at[src, k],
            device_id={"chan": target}, device_id_type=MESH,
        )

    def send_up(d, k):
        return send(index(z - d, y, core), k, up_sem.at[d, k], up)

    def send_down(d, k):
        return send(index(z + d, y, core), k, down_sem.at[d, k], down)

    def send_y(d, k):
        return send(index(z + d, y, core), k, y_sem.at[d + outer - 1, k], y_peer)

    def send_core(far, d, k):
        yy = inner - 1 - y if far else y
        return send(index(z + d, yy, core), k, core_sem.at[far, d + outer - 1, k], core_peer)

    def send_detour(k):
        src = index(z, inner - 1 - y, core)
        return send(src, k, detour_sem.at[k], index(buddy, y, core))

    def in_line(d):
        return jnp.logical_and(z + d >= 0, z + d < outer)

    def arrived(zz, yy, kk, k):
        src = index(zz, yy, kk)
        send(src, k, y_sem.at[0, 0], y_peer if inner > 1 else core_peer).wait_recv()

    for k in range(CHUNKS):
        load(k).wait()
        x = xbuf[rows_of(k)].reshape(sizes[k] * windows, samp)
        sums = jnp.dot(x, tab[...], preferred_element_type=jnp.float32)
        tiles, _, lanes = spec.shape
        for t in range(tiles):
            spec[t, pl.ds(0, sizes[k] * windows), :] = sums[:, t * lanes : (t + 1) * lanes]
        per_tile = lanes // width
        for g in range(nb):
            t, at = g // per_tile, g % per_tile * width
            parts = [spec[t, pl.ds(w, sizes[k], stride=windows), :] for w in range(windows)]
            packed = jnp.concatenate([p[:, at : at + width] for p in parts], axis=1)
            if g < nb - 1:
                xs[g, rows_of(k), :] = packed
            else:
                own[rows_of(k), :] = packed
        if k == 0:
            pl.semaphore_wait(
                barrier,
                nb - 1 + (inner - 1) + (cores - 1) + has_up.astype(jnp.int32) + has_down.astype(jnp.int32),
            )
        for g in range(nb - 1):
            band_copy(g, k).start()

    def own_chunk(k):
        rows = rows_of(k)
        total = own[rows, :]
        for g in range(nb - 1):
            band_copy(g, k).wait_recv()
            total = total + xr[g, rows, :]
        white = []
        for w in range(windows):
            s = total[:, w * width : (w + 1) * width]
            power = jnp.sum(s * s, axis=1, keepdims=True) * (1.0 / width)
            white.append(s * lax.rsqrt(power + 1e-06))
        panel = jnp.concatenate(white, axis=1)
        g_ref[me, rows, :] = panel.astype(jnp.bfloat16)

        @pl.when(has_up)
        def _():
            send_up(0, k).start()

        @pl.when(has_down)
        def _():
            send_down(0, k).start()

        if inner > 1:
            send_y(0, k).start()
        if cores > 1:
            send_core(0, 0, k).start()
        feats = panel.shape[1]
        is_real = lax.broadcasted_iota(jnp.int32, panel.shape, 1) % width < K
        rotated = jnp.where(
            is_real, pltpu.roll(panel, feats - K, axis=1), -pltpu.roll(panel, K, axis=1)
        )
        pq_ref[0, rows, :] = panel.astype(jnp.bfloat16)
        pq_ref[1, rows, :] = rotated.astype(jnp.bfloat16)

    def line_chunk(d, k):
        @pl.when(in_line(d))
        def _():
            arrived(z + d, y, core, k)
            if d < 0:
                pl.when(has_up)(lambda: send_up(-d, k).start())
            else:
                pl.when(has_down)(lambda: send_down(d, k).start())
            if inner > 1:
                if detour and k in DETOUR:
                    pl.when(z + d != buddy)(lambda: send_y(d, k).start())
                else:
                    send_y(d, k).start()
            if cores > 1:
                send_core(0, d, k).start()

    def far_chunk(d, k):
        @pl.when(in_line(d))
        def _():
            arrived(z + d, inner - 1 - y, core, k)
            if d == 0 and detour and k in DETOUR:
                send_detour(k).start()
            if cores > 1:
                send_core(1, d, k).start()

    def gram(src, h):
        first, cols = starts[GROUPS[h][0]], sum(sizes[k] for k in GROUPS[h])
        two, _, feats = pq_ref.shape
        product = lax.dot_general(
            pq_ref[...].reshape(two * chans, feats),
            g_ref[src, pl.ds(first, cols), :],
            (((1,), (1,)), ((), ())),
            preferred_element_type=jnp.float32,
        )
        product = (product * (1.0 / width)).astype(jnp.bfloat16)
        at = pl.ds(pl.multiple_of(src * chans + first, cols), cols)
        for i in range(two):
            o_ref[i, :, at] = product[i * chans : (i + 1) * chans]

    def near_gram(d, h):
        pl.when(in_line(d))(lambda: gram(index(z + d, y, core), h))

    def far_gram(d, h):
        pl.when(in_line(d))(lambda: gram(index(z + d, inner - 1 - y, core), h))

    def peer_gram(far, d, h):
        @pl.when(in_line(d))
        def _():
            yy = inner - 1 - y if far else y
            for k in GROUPS[h]:
                arrived(z + d, yy, cores - 1 - core, k)
            gram(index(z + d, yy, cores - 1 - core), h)

    hop, cost = 1.6, 0.3
    wire = [0.35 * e for e in EIGHTHS]
    moves, jobs = [], []
    near, far = {}, {}
    for k in range(CHUNKS):
        for d in range(outer):
            near[d, k] = 2 * sum(wire[1 : k + 1]) + (hop + wire[k]) * d
    free = 0.0
    for d, k in sorted(near, key=lambda e: (near[e], e)):
        free = max(free, near[d, k]) + wire[k]
        far[d, k] = free + hop
    for (d, k), t in near.items():
        if d == 0:
            moves.append((t, 0, own_chunk, (k,)))
        else:
            moves += [(t, 1, line_chunk, (s, k)) for s in (-d, d)]
    if inner > 1:
        for (d, k), t in far.items():
            moves += [(t, 2, far_chunk, (s, k)) for s in sorted({-d, d})]
    ready = near[0, CHUNKS - 1]
    for h in range(len(GROUPS)):
        last = GROUPS[h][-1]
        for d in range(outer):
            for s in sorted({-d, d}):
                jobs.append((max(ready, near[d, last]), 0, near_gram, (s, h)))
                if inner > 1:
                    jobs.append((max(ready, far[d, last]), 1, far_gram, (s, h)))
                if cores > 1:
                    for f, times in enumerate((near, far)[:inner]):
                        jobs.append((max(ready, times[d, last] + hop), 2, peer_gram, (f, s, h)))
    order = lambda e: (e[0], e[1], e[3])
    moves.sort(key=order)
    jobs.sort(key=order)
    now = 0.0
    for t, _, run, args in moves:
        while jobs and jobs[0][0] <= now and now + cost <= t:
            _, _, job, what = jobs.pop(0)
            job(*what)
            now += cost / 2
        run(*args)
        now = max(now, t)
    for _, _, job, what in jobs:
        job(*what)

    for k in range(CHUNKS):
        for g in range(nb - 1):
            band_copy(g, k).wait_send()
        for d in range(outer):
            pl.when(jnp.logical_and(in_line(-d), has_up))(lambda: send_up(d, k).wait_send())
            pl.when(jnp.logical_and(in_line(d), has_down))(lambda: send_down(d, k).wait_send())
        for d in range(1 - outer, outer):
            @pl.when(in_line(d))
            def _():
                if inner > 1:
                    if detour and k in DETOUR:
                        pl.when(z + d != buddy)(lambda: send_y(d, k).wait_send())
                    else:
                        send_y(d, k).wait_send()
                if d == 0 and detour and k in DETOUR:
                    send_detour(k).wait_send()
                if cores > 1:
                    for far in range(inner):
                        send_core(far, d, k).wait_send()


def cross_spectra(n, nb, strain, band_start):
    chans, windows, samp = strain.shape
    width = 2 * K
    feats = windows * width
    outer = n
    for _ in range(2):
        outer = outer // 2 if outer % 2 == 0 else outer
    dma = pltpu.SemaphoreType.DMA
    return pl.pallas_call(
        functools.partial(gather_kernel, n, nb),
        out_shape=jax.ShapeDtypeStruct((2, chans, n * chans), jnp.bfloat16),
        in_specs=[
            pl.BlockSpec(memory_space=pl.ANY),
            pl.BlockSpec(memory_space=pl.ANY),
        ],
        out_specs=pl.BlockSpec(memory_space=pltpu.VMEM),
        scratch_shapes=[
            pltpu.VMEM((chans, windows, samp), jnp.bfloat16),
            pltpu.VMEM((4, min(64, samp), nb * width), jnp.float32),
            pltpu.VMEM((4, samp // min(64, samp), nb * width), jnp.float32),
            pltpu.VMEM((samp, nb * width), jnp.bfloat16),
            pltpu.VMEM((nb * width // 128, chans * max(EIGHTHS) // 8 * windows, 128), jnp.float32),
            pltpu.VMEM((chans, feats), jnp.float32),
            pltpu.VMEM((nb - 1, chans, feats), jnp.float32),
            pltpu.VMEM((nb - 1, chans, feats), jnp.float32),
            pltpu.VMEM((n, chans, feats), jnp.bfloat16),
            pltpu.VMEM((2, chans, feats), jnp.bfloat16),
            pltpu.SMEM(band_start.shape, jnp.int32),
            dma,
            dma((CHUNKS,)),
            dma((nb - 1, CHUNKS)),
            dma((nb - 1, CHUNKS)),
            dma((outer, CHUNKS)),
            dma((outer, CHUNKS)),
            dma((2 * outer - 1, CHUNKS)),
            dma((2, 2 * outer - 1, CHUNKS)),
            dma((CHUNKS,)),
            dma((n, CHUNKS)),
        ],
        compiler_params=pltpu.CompilerParams(
            collective_id=0, has_side_effects=True, vmem_limit_bytes=48 << 20
        ),
    )(band_start, strain)


def write_kernel(pieces, held, out, sem):
    two, chans, _ = held.shape
    rows = chans // pieces
    copies = []
    for i in range(two):
        for p in range(pieces):
            at = pl.ds(p * rows, rows)
            copies.append(pltpu.make_async_copy(held.at[i, at], out.at[0, i, at], sem.at[i, p]))
    for copy in copies:
        copy.start()
    for copy in copies:
        copy.wait()


def write_out(held):
    pieces = 8
    return pl.pallas_call(
        functools.partial(write_kernel, pieces),
        out_shape=jax.ShapeDtypeStruct((1,) + held.shape, held.dtype),
        in_specs=[pl.BlockSpec(memory_space=pl.ANY)],
        out_specs=pl.BlockSpec(memory_space=pl.ANY),
        scratch_shapes=[pltpu.SemaphoreType.DMA((held.shape[0], pieces))],
        compiler_params=pltpu.CompilerParams(vmem_limit_bytes=1 << 20),
    )(held)


def shards(n, nb, strain, band_start):
    return write_out(cross_spectra(n, nb, strain, band_start))


def solution(mesh):
    return jax.shard_map(
        functools.partial(shards, mesh.shape["chan"], mesh.shape["band"]),
        mesh=mesh,
        in_specs=(P("chan", None, "band"), P()),
        out_specs=P("band", None, "chan", None),
        check_vma=False,
    )
```

```python
import functools
import math

import jax
import jax.numpy as jnp
from jax import lax
from jax.experimental import pallas as pl
from jax.experimental.pallas import tpu as pltpu
from jax.sharding import PartitionSpec as P

WINDOW_SAMPLES = 4096
K = 32
EIGHTHS = (2, 2, 2, 2)
CHUNKS = len(EIGHTHS)
GROUPS = ((0, 1, 2, 3),)
DETOUR = (1, 3)
MESH = pl.DeviceIdType.MESH


def cos_turns(m):
    half, quarter = WINDOW_SAMPLES // 2, WINDOW_SAMPLES // 4
    t = (jnp.abs(m - half) - quarter).astype(jnp.float32) * (math.pi / half)
    z = t * t
    p = jnp.float32(1.0 / math.factorial(13))
    for order in (11, 9, 7, 5, 3, 1):
        sign = 1.0 if order % 4 == 1 else -1.0
        p = p * z + jnp.float32(sign / math.factorial(order))
    return p * t


def gather_kernel(
    n, nb, start_hbm, x_hbm, o_ref,
    xbuf, trig, bases, tab, spec, own, xs, xr, g_ref, pq_ref,
    start_ref, start_sem, in_sem, xs_sem, xr_sem, up_sem, down_sem, y_sem, core_sem, detour_sem, recv_sem,
):
    chans, windows, samp = xbuf.shape
    width = 2 * K
    sizes = [chans * e // 8 for e in EIGHTHS]
    starts = [sum(sizes[:k]) for k in range(CHUNKS)]

    def rows_of(k):
        return pl.ds(starts[k], sizes[k])

    cores = 2 if n % 2 == 0 else 1
    chips = n // cores
    inner = 2 if chips % 2 == 0 else 1
    outer = chips // inner
    me = lax.axis_index("chan")
    band = lax.axis_index("band")
    core = lax.rem(me, cores)
    chip = lax.div(me, cores)
    y = lax.rem(chip, inner)
    z = lax.div(chip, inner)

    def index(zz, yy, kk):
        return (zz * inner + yy) * cores + kk

    detour = inner > 1 and outer % 2 == 0
    buddy = z + 1 - 2 * lax.rem(z, 2)

    def load(k):
        rows = rows_of(k)
        return pltpu.make_async_copy(x_hbm.at[rows], xbuf.at[rows], in_sem.at[k])

    for k in range(CHUNKS):
        load(k).start()
    first_bins = pltpu.make_async_copy(start_hbm, start_ref, start_sem)
    first_bins.start()

    barrier = pltpu.get_barrier_semaphore()
    up, down = index(z + 1, y, core), index(z - 1, y, core)
    y_peer, core_peer = index(z, inner - 1 - y, core), index(z, y, cores - 1 - core)
    has_up, has_down = z < outer - 1, z > 0
    for g in range(nb - 1):
        pl.semaphore_signal(
            barrier, inc=1, device_id={"band": lax.rem(band + 1 + g, nb)}, device_id_type=MESH
        )

    @pl.when(has_up)
    def _():
        pl.semaphore_signal(barrier, inc=1, device_id={"chan": up}, device_id_type=MESH)

    @pl.when(has_down)
    def _():
        pl.semaphore_signal(barrier, inc=1, device_id={"chan": down}, device_id_type=MESH)

    if inner > 1:
        pl.semaphore_signal(barrier, inc=1, device_id={"chan": y_peer}, device_id_type=MESH)
    if cores > 1:
        pl.semaphore_signal(barrier, inc=1, device_id={"chan": core_peer}, device_id_type=MESH)

    first_bins.wait()
    lane = lax.broadcasted_iota(jnp.int32, (1, nb * width), 1)
    freq = lane % K
    for g in range(nb):
        freq = freq + jnp.where(lane // width == g, start_ref[lax.rem(band + 1 + g, nb)], 0)
    shift = jnp.where((lane // K) % 2 == 1, WINDOW_SAMPLES // 4, 0)
    step = trig.shape[1]
    steps = samp // step
    offset = lax.broadcasted_iota(jnp.int32, (step, nb * width), 0)
    base = band * samp + step * lax.broadcasted_iota(jnp.int32, (steps, nb * width), 0)
    wrap, lag = WINDOW_SAMPLES - 1, 3 * (WINDOW_SAMPLES // 4)
    angle = offset * freq + shift
    trig[0] = cos_turns(angle & wrap)
    trig[1] = cos_turns((angle + lag) & wrap)
    trig[2] = 0.5 * cos_turns(offset & wrap)
    trig[3] = 0.5 * cos_turns((offset + lag) & wrap)
    angle = base * freq
    bases[0] = cos_turns(angle & wrap)
    bases[1] = cos_turns((angle + lag) & wrap)
    bases[2] = cos_turns(base & wrap)
    bases[3] = cos_turns((base + lag) & wrap)

    def fill(r, carry):
        turn = [bases[i, pl.ds(r, 1), :] for i in range(4)]
        taper = 0.5 - (trig[2] * turn[2] - trig[3] * turn[3])
        wave = trig[0] * turn[0] - trig[1] * turn[1]
        tab[pl.ds(pl.multiple_of(r * step, step), step), :] = (taper * wave).astype(jnp.bfloat16)
        return carry

    lax.fori_loop(0, steps, fill, 0, unroll=2)

    def band_copy(g, k):
        return pltpu.make_async_remote_copy(
            src_ref=xs.at[g, rows_of(k)],
            dst_ref=xr.at[g, rows_of(k)],
            send_sem=xs_sem.at[g, k],
            recv_sem=xr_sem.at[g, k],
            device_id={"band": lax.rem(band + 1 + g, nb)},
            device_id_type=MESH,
        )

    def send(src, k, sem, target):
        slot = g_ref.at[src, rows_of(k)]
        return pltpu.make_async_remote_copy(
            src_ref=slot, dst_ref=slot, send_sem=sem, recv_sem=recv_sem.at[src, k],
            device_id={"chan": target}, device_id_type=MESH,
        )

    def send_up(d, k):
        return send(index(z - d, y, core), k, up_sem.at[d, k], up)

    def send_down(d, k):
        return send(index(z + d, y, core), k, down_sem.at[d, k], down)

    def send_y(d, k):
        return send(index(z + d, y, core), k, y_sem.at[d + outer - 1, k], y_peer)

    def send_core(far, d, k):
        yy = inner - 1 - y if far else y
        return send(index(z + d, yy, core), k, core_sem.at[far, d + outer - 1, k], core_peer)

    def send_detour(k):
        src = index(z, inner - 1 - y, core)
        return send(src, k, detour_sem.at[k], index(buddy, y, core))

    def in_line(d):
        return jnp.logical_and(z + d >= 0, z + d < outer)

    def arrived(zz, yy, kk, k):
        src = index(zz, yy, kk)
        send(src, k, y_sem.at[0, 0], y_peer if inner > 1 else core_peer).wait_recv()

    for k in range(CHUNKS):
        load(k).wait()
        x = xbuf[rows_of(k)].reshape(sizes[k] * windows, samp)
        sums = jnp.dot(x, tab[...], preferred_element_type=jnp.float32)
        tiles, _, lanes = spec.shape
        for t in range(tiles):
            spec[t, pl.ds(0, sizes[k] * windows), :] = sums[:, t * lanes : (t + 1) * lanes]
        per_tile = lanes // width
        for g in range(nb):
            t, at = g // per_tile, g % per_tile * width
            parts = [spec[t, pl.ds(w, sizes[k], stride=windows), :] for w in range(windows)]
            packed = jnp.concatenate([p[:, at : at + width] for p in parts], axis=1)
            if g < nb - 1:
                xs[g, rows_of(k), :] = packed
            else:
                own[rows_of(k), :] = packed
        if k == 0:
            pl.semaphore_wait(
                barrier,
                nb - 1 + (inner - 1) + (cores - 1) + has_up.astype(jnp.int32) + has_down.astype(jnp.int32),
            )
        for g in range(nb - 1):
            band_copy(g, k).start()

    def own_chunk(k):
        rows = rows_of(k)
        total = own[rows, :]
        for g in range(nb - 1):
            band_copy(g, k).wait_recv()
            total = total + xr[g, rows, :]
        white = []
        for w in range(windows):
            s = total[:, w * width : (w + 1) * width]
            power = jnp.sum(s * s, axis=1, keepdims=True) * (1.0 / width)
            white.append(s * lax.rsqrt(power + 1e-06))
        panel = jnp.concatenate(white, axis=1)
        g_ref[me, rows, :] = panel.astype(jnp.bfloat16)

        @pl.when(has_up)
        def _():
            send_up(0, k).start()

        @pl.when(has_down)
        def _():
            send_down(0, k).start()

        if inner > 1:
            send_y(0, k).start()
        if cores > 1:
            send_core(0, 0, k).start()
        feats = panel.shape[1]
        is_real = lax.broadcasted_iota(jnp.int32, panel.shape, 1) % width < K
        rotated = jnp.where(
            is_real, pltpu.roll(panel, feats - K, axis=1), -pltpu.roll(panel, K, axis=1)
        )
        pq_ref[0, rows, :] = panel.astype(jnp.bfloat16)
        pq_ref[1, rows, :] = rotated.astype(jnp.bfloat16)

    def line_chunk(d, k):
        @pl.when(in_line(d))
        def _():
            arrived(z + d, y, core, k)
            if d < 0:
                pl.when(has_up)(lambda: send_up(-d, k).start())
            else:
                pl.when(has_down)(lambda: send_down(d, k).start())
            if inner > 1:
                if detour and k in DETOUR:
                    pl.when(z + d != buddy)(lambda: send_y(d, k).start())
                else:
                    send_y(d, k).start()
            if cores > 1:
                send_core(0, d, k).start()

    def far_chunk(d, k):
        @pl.when(in_line(d))
        def _():
            arrived(z + d, inner - 1 - y, core, k)
            if d == 0 and detour and k in DETOUR:
                send_detour(k).start()
            if cores > 1:
                send_core(1, d, k).start()

    def gram(src, h):
        first, cols = starts[GROUPS[h][0]], sum(sizes[k] for k in GROUPS[h])
        two, _, feats = pq_ref.shape
        product = lax.dot_general(
            pq_ref[...].reshape(two * chans, feats),
            g_ref[src, pl.ds(first, cols), :],
            (((1,), (1,)), ((), ())),
            preferred_element_type=jnp.float32,
        )
        product = (product * (1.0 / width)).astype(jnp.bfloat16)
        at = pl.ds(pl.multiple_of(src * chans + first, cols), cols)
        for i in range(two):
            o_ref[i, :, at] = product[i * chans : (i + 1) * chans]

    def near_gram(d, h):
        pl.when(in_line(d))(lambda: gram(index(z + d, y, core), h))

    def far_gram(d, h):
        pl.when(in_line(d))(lambda: gram(index(z + d, inner - 1 - y, core), h))

    def peer_gram(far, d, h):
        @pl.when(in_line(d))
        def _():
            yy = inner - 1 - y if far else y
            for k in GROUPS[h]:
                arrived(z + d, yy, cores - 1 - core, k)
            gram(index(z + d, yy, cores - 1 - core), h)

    hop, cost = 1.6, 0.3
    wire = [0.35 * e for e in EIGHTHS]
    moves, jobs = [], []
    near, far = {}, {}
    for k in range(CHUNKS):
        for d in range(outer):
            near[d, k] = 2 * sum(wire[1 : k + 1]) + (hop + wire[k]) * d
    free = 0.0
    for d, k in sorted(near, key=lambda e: (near[e], e)):
        free = max(free, near[d, k]) + wire[k]
        far[d, k] = free + hop
    for (d, k), t in near.items():
        if d == 0:
            moves.append((t, 0, own_chunk, (k,)))
        else:
            moves += [(t, 1, line_chunk, (s, k)) for s in (-d, d)]
    if inner > 1:
        for (d, k), t in far.items():
            moves += [(t, 2, far_chunk, (s, k)) for s in sorted({-d, d})]
    ready = near[0, CHUNKS - 1]
    for h in range(len(GROUPS)):
        last = GROUPS[h][-1]
        for d in range(outer):
            for s in sorted({-d, d}):
                jobs.append((max(ready, near[d, last]), 0, near_gram, (s, h)))
                if inner > 1:
                    jobs.append((max(ready, far[d, last]), 1, far_gram, (s, h)))
                if cores > 1:
                    for f, times in enumerate((near, far)[:inner]):
                        jobs.append((max(ready, times[d, last] + hop), 2, peer_gram, (f, s, h)))
    order = lambda e: (e[0], e[1], e[3])
    moves.sort(key=order)
    jobs.sort(key=order)
    now = 0.0
    for t, _, run, args in moves:
        while jobs and jobs[0][0] <= now and now + cost <= t:
            _, _, job, what = jobs.pop(0)
            job(*what)
            now += cost / 2
        run(*args)
        now = max(now, t)
    for _, _, job, what in jobs:
        job(*what)

    for k in range(CHUNKS):
        for g in range(nb - 1):
            band_copy(g, k).wait_send()
        for d in range(outer):
            pl.when(jnp.logical_and(in_line(-d), has_up))(lambda: send_up(d, k).wait_send())
            pl.when(jnp.logical_and(in_line(d), has_down))(lambda: send_down(d, k).wait_send())
        for d in range(1 - outer, outer):
            @pl.when(in_line(d))
            def _():
                if inner > 1:
                    if detour and k in DETOUR:
                        pl.when(z + d != buddy)(lambda: send_y(d, k).wait_send())
                    else:
                        send_y(d, k).wait_send()
                if d == 0 and detour and k in DETOUR:
                    send_detour(k).wait_send()
                if cores > 1:
                    for far in range(inner):
                        send_core(far, d, k).wait_send()


def cross_spectra(n, nb, strain, band_start):
    chans, windows, samp = strain.shape
    width = 2 * K
    feats = windows * width
    outer = n
    for _ in range(2):
        outer = outer // 2 if outer % 2 == 0 else outer
    dma = pltpu.SemaphoreType.DMA
    return pl.pallas_call(
        functools.partial(gather_kernel, n, nb),
        out_shape=jax.ShapeDtypeStruct((2, chans, n * chans), jnp.bfloat16),
        in_specs=[
            pl.BlockSpec(memory_space=pl.ANY),
            pl.BlockSpec(memory_space=pl.ANY),
        ],
        out_specs=pl.BlockSpec(memory_space=pltpu.VMEM),
        scratch_shapes=[
            pltpu.VMEM((chans, windows, samp), jnp.bfloat16),
            pltpu.VMEM((4, min(64, samp), nb * width), jnp.float32),
            pltpu.VMEM((4, samp // min(64, samp), nb * width), jnp.float32),
            pltpu.VMEM((samp, nb * width), jnp.bfloat16),
            pltpu.VMEM((nb * width // 128, chans * max(EIGHTHS) // 8 * windows, 128), jnp.float32),
            pltpu.VMEM((chans, feats), jnp.float32),
            pltpu.VMEM((nb - 1, chans, feats), jnp.float32),
            pltpu.VMEM((nb - 1, chans, feats), jnp.float32),
            pltpu.VMEM((n, chans, feats), jnp.bfloat16),
            pltpu.VMEM((2, chans, feats), jnp.bfloat16),
            pltpu.SMEM(band_start.shape, jnp.int32),
            dma,
            dma((CHUNKS,)),
            dma((nb - 1, CHUNKS)),
            dma((nb - 1, CHUNKS)),
            dma((outer, CHUNKS)),
            dma((outer, CHUNKS)),
            dma((2 * outer - 1, CHUNKS)),
            dma((2, 2 * outer - 1, CHUNKS)),
            dma((CHUNKS,)),
            dma((n, CHUNKS)),
        ],
        compiler_params=pltpu.CompilerParams(
            collective_id=0, has_side_effects=True, vmem_limit_bytes=48 << 20
        ),
    )(band_start, strain)


def write_kernel(pieces, held, out, sem):
    two, chans, _ = held.shape
    rows = chans // pieces
    copies = []
    for i in range(two):
        for p in range(pieces):
            at = pl.ds(p * rows, rows)
            copies.append(pltpu.make_async_copy(held.at[i, at], out.at[0, i, at], sem.at[i, p]))
    for copy in copies:
        copy.start()
    for copy in copies:
        copy.wait()


def write_out(held):
    pieces = 8
    return pl.pallas_call(
        functools.partial(write_kernel, pieces),
        out_shape=jax.ShapeDtypeStruct((1,) + held.shape, held.dtype),
        in_specs=[pl.BlockSpec(memory_space=pl.ANY)],
        out_specs=pl.BlockSpec(memory_space=pl.ANY),
        scratch_shapes=[pltpu.SemaphoreType.DMA((held.shape[0], pieces))],
        compiler_params=pltpu.CompilerParams(vmem_limit_bytes=1 << 20),
    )(held)


def shards(n, nb, strain, band_start):
    return write_out(cross_spectra(n, nb, strain, band_start))


def solution(mesh):
    return jax.shard_map(
        functools.partial(shards, mesh.shape["chan"], mesh.shape["band"]),
        mesh=mesh,
        in_specs=(P("chan", None, "band"), P()),
        out_specs=P("band", None, "chan", None),
        check_vma=False,
    )
```
